32 devices in a mesh: batch: 4 (over x, core), hidden: 4 (over z), solver: 2 (over y).
Axes of the slice: x: 2, y: 2, z: 4, core: 2. Of those that a mesh axis runs over, the one named last changes fastest.
Arguments:
- activations: bfloat16 [1024, 4096], P('batch', ('hidden', 'solver')), may hold values from -16 to 16, as said below
- cotangent: bfloat16 [8192, 1024], P(('hidden', 'solver'), 'batch'), may hold values from -0.1875 to 0.1875
- weight: bfloat16 [4096, 8192], P(('hidden', 'solver'), 'batch'), may hold values from -0.09375 to 0.09375
- left_old: float32 [4, 8, 1024, 1024], P('hidden', 'batch'), may hold values from -0.001953125 to 2.0019531, as said below
- right_old: float32 [4, 8, 1024, 1024], P('hidden', 'batch'), may hold values from -0.001953125 to 2.0019531, as said below
Outputs:
- first_out: bfloat16 [8192, 1024], P(('hidden', 'solver'), 'batch')
- new_left: float32 [4, 8, 1024, 1024], P('hidden', 'batch', 'solver')
- new_right: float32 [4, 8, 1024, 1024], P('hidden', 'batch', 'solver')
- direction: float32 [4096, 8192], P(('hidden', 'solver'), 'batch')
- second_out: bfloat16 [8192, 1024], P(('hidden', 'solver'), 'batch')
The draws below stay inside these ranges and needn't reach their ends.
Inputs may be any that keep to these rules, and one draw needn't show every extreme that they name: `activations`: in the hidden draw each feature carries its own scale. `left_old`: every block is symmetric, its diagonal is positive and larger than the sum of the magnitudes of the rest of its row. `right_old`: every block is symmetric, its diagonal is positive and larger than the sum of the magnitudes of the rest of its row.
All inputs are finite; a program needn't handle non-finite values. Where the reference program divides by a largest or mean magnitude, that divisor is 1e-20 or more.
Results may differ from the reference program's by a relative error of at most 0.017.
Values may be sent and summed in bfloat16 or wider, within the bound.
A program may use at most 128 MiB of HBM per device.

```python
import jax
import jax.numpy as jnp
from jax import lax

DIN = 4096
DOUT = 8192
BLOCK = 1024
TOK_DEV = 256
TOKENS = 1024
NROW = 4
NCOL = 8
N_BATCH = 4


def draw_activations(key, part):
    values = jnp.clip(jax.random.normal(jax.random.fold_in(key, 11), (TOKENS, DIN), jnp.float32), -4.0, 4.0)
    return values.astype(jnp.bfloat16)


def factor_blocks(key):
    diagonal = jnp.exp(jax.random.uniform(jax.random.fold_in(key, 21), (NROW, NCOL, BLOCK), jnp.float32, jnp.log(0.5), jnp.log(2.0)))
    off_part = jnp.clip(jax.random.normal(jax.random.fold_in(key, 22), (NROW, NCOL, BLOCK, BLOCK), jnp.float32), -4.0, 4.0) * (0.5 / BLOCK)
    symmetric = 0.5 * (off_part + jnp.swapaxes(off_part, 2, 3))
    identity = jnp.eye(BLOCK, dtype=jnp.float32)
    return symmetric * (1.0 - identity) + diagonal[..., None] * identity


def draw_left_old(key, part):
    return factor_blocks(jax.random.fold_in(key, 1))


def draw_right_old(key, part):
    return factor_blocks(jax.random.fold_in(key, 2))


def block_scale(stream_key, shape, shards, least, high):
    factor_of, own = 1.0, jax.random.fold_in(stream_key, 6)
    for axis_at, shards_of in shards:
        heights = jnp.exp(jax.random.uniform(jax.random.fold_in(own, axis_at), (shards_of,), jnp.float32, least / len(shards), high / len(shards)))
        factor_of = factor_of * jnp.repeat(heights, shape[axis_at] // shards_of).reshape([-1 if axis == axis_at else 1 for axis in range(len(shape))])
    return factor_of


def normal_values(stream_key, extent, scale, most, split=(), kind=jnp.bfloat16):
    entries = jax.random.normal(stream_key, extent, jnp.float32) * scale
    if len(split) > 0:
        entries = block_scale(stream_key, extent, split, -0.22, 0.18) * entries
    return jnp.clip(entries, min=-most, max=most).astype(kind)


def setup_inputs(seed: int = 0) -> dict:
    splits = jax.random.split(jax.random.key(seed), 6)
    return {
        "activations": draw_activations(jax.random.fold_in(splits[5], 71), 0),
        "cotangent": normal_values(splits[1], (DOUT, TOKENS), (TOKENS ** -0.5), 0.1875, ((0, 8), (1, 4))),
        "weight": normal_values(splits[2], (DIN, DOUT), DIN ** -0.5, 0.09375, ((0, 8), (1, 4))),
        "left_old": draw_left_old(jax.random.fold_in(splits[5], 71), 0),
        "right_old": draw_right_old(jax.random.fold_in(splits[5], 71), 0),
    }


STAT_DECAY = 0.8
LEARN_RATE = 0.005
EPSILON = 1e-06

def product(left_mat, right_mat):
    return jnp.dot(left_mat, right_mat, precision=lax.Precision.HIGHEST, preferred_element_type=jnp.float32)

def inverse_root(factor):
    identity = jnp.eye(BLOCK, dtype=jnp.float32)
    scaled = 2.5 / (jnp.max(lax.optimization_barrier(jnp.sum(jnp.abs(factor), axis=1))) + EPSILON)
    moment = scaled * factor
    newton_step = (5.0 * identity - moment) * 0.25
    power_term = product(product(product(product(newton_step, newton_step), newton_step), newton_step), moment)
    next_step = (5.0 * identity - power_term) * 0.25
    return scaled ** 0.25 * product(newton_step, next_step)

def forward(activations, weight):
    outputs = lax.dot_general(weight, activations, (((0,), (1,)), ((), ())), preferred_element_type=jnp.float32)
    return outputs.astype(jnp.bfloat16)

def per_block(inputs):
    grad_block, left_block, right_block = inputs
    gram_left = lax.dot_general(grad_block, grad_block, (((0,), (0,)), ((), ())), preferred_element_type=jnp.float32)
    gram_right = lax.dot_general(grad_block, grad_block, (((1,), (1,)), ((), ())), preferred_element_type=jnp.float32)
    left_new = STAT_DECAY * left_block + (1.0 - STAT_DECAY) / BLOCK * gram_left
    right_new = STAT_DECAY * right_block + (1.0 - STAT_DECAY) / BLOCK * gram_right
    grad_float = grad_block.astype(jnp.float32).T
    mixed_rows = product(inverse_root(left_new), grad_float)
    update = product(mixed_rows, inverse_root(right_new))
    spread = jnp.sqrt(jnp.mean(update * update) + EPSILON)
    return (left_new, right_new, update / spread)

def reference(activations, cotangent, weight, left_old, right_old):
    first_out = forward(activations, weight)

    def add_group(carry, group):
        acts = lax.dynamic_slice_in_dim(activations, (group * TOK_DEV).astype(jnp.int32), TOK_DEV, 0)
        cotan = lax.dynamic_slice_in_dim(cotangent, (group * TOK_DEV).astype(jnp.int32), TOK_DEV, 1)
        partial_grad = jnp.dot(cotan, acts, preferred_element_type=jnp.float32)
        return (carry + partial_grad.astype(jnp.bfloat16).astype(jnp.float32), None)
    grad_sum, _ = lax.scan(add_group, jnp.zeros((DOUT, DIN), jnp.float32), jnp.arange(N_BATCH, dtype=jnp.int32))
    grad = grad_sum.astype(jnp.bfloat16)
    blocks = grad.reshape(NCOL, BLOCK, NROW, BLOCK).transpose(2, 0, 1, 3).reshape(NROW * NCOL, BLOCK, BLOCK)
    lefts = left_old.reshape(NROW * NCOL, BLOCK, BLOCK)
    rights = right_old.reshape(NROW * NCOL, BLOCK, BLOCK)
    new_left, new_right, updates = lax.map(per_block, (blocks, lefts, rights))
    new_left = new_left.reshape(NROW, NCOL, BLOCK, BLOCK)
    new_right = new_right.reshape(NROW, NCOL, BLOCK, BLOCK)
    direction = updates.reshape(NROW, NCOL, BLOCK, BLOCK).transpose(0, 2, 1, 3).reshape(DIN, DOUT)
    new_weight = (weight.astype(jnp.float32) - LEARN_RATE * direction).astype(jnp.bfloat16)
    second_out = forward(activations, new_weight)
    return (first_out, new_left, new_right, direction, second_out)
```

```python
import jax
import jax.numpy as jnp
from jax import lax
from jax.sharding import PartitionSpec as P

BLOCK = 1024


STAT_DECAY = 0.8
LEARN_RATE = 0.005
EPSILON = 1e-06

ALL = ("batch", "hidden", "solver")
FEATURES = ("hidden", "solver")


def product(left_mat, right_mat):
    return jnp.einsum("bij,bjk->bik", left_mat, right_mat, preferred_element_type=jnp.float32)


def prepare(factor):
    identity = jnp.eye(BLOCK, dtype=jnp.float32)
    scaled = 2.5 / (jnp.max(jnp.sum(jnp.abs(factor), axis=2), axis=1) + EPSILON)
    moment = scaled[:, None, None] * factor
    newton_step = (5.0 * identity - moment) * 0.25
    return (scaled, moment.astype(jnp.bfloat16), newton_step.astype(jnp.bfloat16))


def apply_root(start, moment, step):
    power = start
    for _ in range(4):
        power = product(power.astype(jnp.bfloat16), step)
    power = product(power.astype(jnp.bfloat16), moment)
    return (5.0 * start.astype(jnp.float32) - power) * 0.25


def body(activations, cotangent, weight, left_old, right_old, *, n_batch, n_feat):
    rows_here = weight.shape[0]
    nblocks = weight.shape[1] // BLOCK
    per_batch = n_feat // n_batch
    out_rows = weight.shape[1] // per_batch
    tokens = activations.shape[0]
    to_owner = [
        (b * n_feat + c * n_batch + t, t * n_feat + b * per_batch + c)
        for b in range(n_batch)
        for c in range(per_batch)
        for t in range(n_batch)
    ]
    from_owner = [(target, source) for source, target in to_owner]

    def partial_forward(weight_here):
        split = weight_here.reshape(rows_here, per_batch, out_rows)
        out = jnp.einsum("fco,btf->cbot", split, acts_all, preferred_element_type=jnp.float32)
        return out.astype(jnp.bfloat16).reshape(n_feat * out_rows, tokens)

    def reduce_forward(partial):
        return lax.psum_scatter(partial, FEATURES, scatter_dimension=0, tiled=True)

    acts_all = lax.all_gather(activations, "batch", axis=0, tiled=False)
    acts_block = lax.all_gather(acts_all, "solver", axis=2, tiled=True)
    cot_moved = lax.ppermute(cotangent, ALL, from_owner)
    cot_all = lax.all_gather(cot_moved, FEATURES, axis=0, tiled=False)
    cot_all = cot_all.reshape(per_batch, n_batch, out_rows, tokens)
    first_partial = partial_forward(weight)
    first_partial, cot_all = lax.optimization_barrier((first_partial, cot_all))
    first_sum = reduce_forward(first_partial)
    grad_full = jnp.einsum("cbot,btf->cof", cot_all, acts_block, preferred_element_type=jnp.float32)
    grad_full = grad_full.astype(jnp.bfloat16).reshape(nblocks, BLOCK, BLOCK)
    gram_left = jnp.einsum("bnm,bnk->bmk", grad_full, grad_full, preferred_element_type=jnp.float32)
    gram_right = jnp.einsum(
        "bnm,bkm->bnk", grad_full, grad_full, preferred_element_type=jnp.float32
    )
    left_all = STAT_DECAY * left_old[0] + (1.0 - STAT_DECAY) / BLOCK * gram_left
    right_all = STAT_DECAY * right_old[0] + (1.0 - STAT_DECAY) / BLOCK * gram_right
    first_row = lax.axis_index("solver") * rows_here
    new_left = lax.dynamic_slice_in_dim(left_all, first_row, rows_here, 1)[None]
    new_right = lax.dynamic_slice_in_dim(right_all, first_row, rows_here, 1)[None]
    scale_left, moment_left, step_left = prepare(left_all)
    own_rows = lax.dynamic_slice_in_dim(step_left, first_row, rows_here, 1)
    root_rows = apply_root(own_rows, moment_left, step_left)
    mixed_rows = jnp.einsum(
        "brm,bnm->brn",
        root_rows.astype(jnp.bfloat16),
        grad_full,
        preferred_element_type=jnp.float32,
    )
    scale_right, moment_right, step_right = prepare(right_all)
    turned = product(mixed_rows.astype(jnp.bfloat16), step_right)
    scale_both = (scale_left**0.25) * (scale_right**0.25)
    update = scale_both[:, None, None] * apply_root(turned, moment_right, step_right)
    update, first_sum = lax.optimization_barrier((update, first_sum))
    first_out = lax.ppermute(first_sum, ALL, to_owner)
    squares = lax.psum(jnp.sum(update * update, axis=(1, 2)), "solver")
    spread = jnp.sqrt(squares / (BLOCK * BLOCK) + EPSILON)
    scaled_update = update / spread[:, None, None]
    direction = jnp.transpose(scaled_update, (1, 0, 2)).reshape(rows_here, nblocks * BLOCK)
    new_weight = (weight.astype(jnp.float32) - LEARN_RATE * direction).astype(jnp.bfloat16)
    second_sum = reduce_forward(partial_forward(new_weight))
    second_out = lax.ppermute(second_sum, ALL, to_owner)
    return (first_out, new_left, new_right, direction, second_out)


def solution(mesh):
    in_specs = (
        P("batch", ("hidden", "solver")),
        P(("hidden", "solver"), "batch"),
        P(("hidden", "solver"), "batch"),
        P("hidden", "batch", None, None),
        P("hidden", "batch", None, None),
    )
    out_specs = (
        P(("hidden", "solver"), "batch"),
        P("hidden", "batch", "solver", None),
        P("hidden", "batch", "solver", None),
        P(("hidden", "solver"), "batch"),
        P(("hidden", "solver"), "batch"),
    )
    n_batch = mesh.shape["batch"]
    n_feat = mesh.shape["hidden"] * mesh.shape["solver"]

    def step(activations, cotangent, weight, left_old, right_old):
        return body(
            activations, cotangent, weight, left_old, right_old, n_batch=n_batch, n_feat=n_feat
        )

    return jax.shard_map(step, mesh=mesh, in_specs=in_specs, out_specs=out_specs, check_vma=False)
```

```python
import jax
import jax.numpy as jnp
from jax import lax
from jax.sharding import PartitionSpec as P

BLOCK = 1024


STAT_DECAY = 0.8
LEARN_RATE = 0.005
EPSILON = 1e-06

ALL = ("batch", "hidden", "solver")
FEATURES = ("hidden", "solver")


def product(left_mat, right_mat):
    return jnp.einsum("bij,bjk->bik", left_mat, right_mat, preferred_element_type=jnp.float32)


def prepare(factor):
    identity = jnp.eye(BLOCK, dtype=jnp.float32)
    scaled = 2.5 / (jnp.max(jnp.sum(jnp.abs(factor), axis=2), axis=1) + EPSILON)
    moment = scaled[:, None, None] * factor
    newton_step = (5.0 * identity - moment) * 0.25
    return (scaled, moment.astype(jnp.bfloat16), newton_step.astype(jnp.bfloat16))


def apply_root(start, moment, step):
    power = start
    for _ in range(4):
        power = product(power.astype(jnp.bfloat16), step)
    power = product(power.astype(jnp.bfloat16), moment)
    return (5.0 * start.astype(jnp.float32) - power) * 0.25


def body(activations, cotangent, weight, left_old, right_old, *, n_batch, n_solver, n_feat):
    rows_here = weight.shape[0]
    nblocks = weight.shape[1] // BLOCK
    per_batch = n_feat // n_batch
    out_rows = weight.shape[1] // per_batch
    tokens = activations.shape[0]
    to_owner = [
        (b * n_feat + c * n_batch + t, t * n_feat + b * per_batch + c)
        for b in range(n_batch)
        for c in range(per_batch)
        for t in range(n_batch)
    ]
    from_owner = [(target, source) for source, target in to_owner]

    def partial_forward(weight_here):
        split = weight_here.reshape(rows_here, per_batch, out_rows)
        out = jnp.einsum("fco,btf->cbot", split, acts_all, preferred_element_type=jnp.float32)
        return out.astype(jnp.bfloat16).reshape(n_feat * out_rows, tokens)

    def reduce_forward(partial):
        return lax.psum_scatter(partial, FEATURES, scatter_dimension=0, tiled=True)

    acts_all = lax.all_gather(activations, "batch", axis=0, tiled=False)
    here = lax.axis_index("solver")
    acts_block = jnp.zeros((n_batch, tokens, n_solver * rows_here), acts_all.dtype)
    for shift in range(n_solver):
        part = acts_all
        if shift > 0:
            pairs = [(at, (at + shift) % n_solver) for at in range(n_solver)]
            part = lax.ppermute(acts_all, "solver", pairs)
        first_col = lax.rem(here + n_solver - shift, n_solver) * rows_here
        acts_block = lax.dynamic_update_slice_in_dim(acts_block, part, first_col, 2)
    cot_moved = lax.ppermute(cotangent, ALL, from_owner)
    cot_all = lax.all_gather(cot_moved, FEATURES, axis=0, tiled=False)
    cot_all = cot_all.reshape(per_batch, n_batch, out_rows, tokens)
    first_partial = partial_forward(weight)
    first_partial, cot_all = lax.optimization_barrier((first_partial, cot_all))
    first_sum = reduce_forward(first_partial)
    grad_full = jnp.einsum("cbot,btf->cof", cot_all, acts_block, preferred_element_type=jnp.float32)
    grad_full = grad_full.astype(jnp.bfloat16).reshape(nblocks, BLOCK, BLOCK)
    gram_left = jnp.einsum("bnm,bnk->bmk", grad_full, grad_full, preferred_element_type=jnp.float32)
    gram_right = jnp.einsum(
        "bnm,bkm->bnk", grad_full, grad_full, preferred_element_type=jnp.float32
    )
    left_all = STAT_DECAY * left_old[0] + (1.0 - STAT_DECAY) / BLOCK * gram_left
    right_all = STAT_DECAY * right_old[0] + (1.0 - STAT_DECAY) / BLOCK * gram_right
    first_row = lax.axis_index("solver") * rows_here
    new_left = lax.dynamic_slice_in_dim(left_all, first_row, rows_here, 1)[None]
    new_right = lax.dynamic_slice_in_dim(right_all, first_row, rows_here, 1)[None]
    scale_left, moment_left, step_left = prepare(left_all)
    own_rows = lax.dynamic_slice_in_dim(step_left, first_row, rows_here, 1)
    root_rows = apply_root(own_rows, moment_left, step_left)
    mixed_rows = jnp.einsum(
        "brm,bnm->brn",
        root_rows.astype(jnp.bfloat16),
        grad_full,
        preferred_element_type=jnp.float32,
    )
    scale_right, moment_right, step_right = prepare(right_all)
    turned = product(mixed_rows.astype(jnp.bfloat16), step_right)
    scale_both = (scale_left**0.25) * (scale_right**0.25)
    update = scale_both[:, None, None] * apply_root(turned, moment_right, step_right)
    update, first_sum = lax.optimization_barrier((update, first_sum))
    first_out = lax.ppermute(first_sum, ALL, to_owner)
    squares = lax.psum(jnp.sum(update * update, axis=(1, 2)), "solver")
    spread = jnp.sqrt(squares / (BLOCK * BLOCK) + EPSILON)
    scaled_update = update / spread[:, None, None]
    direction = jnp.transpose(scaled_update, (1, 0, 2)).reshape(rows_here, nblocks * BLOCK)
    new_weight = (weight.astype(jnp.float32) - LEARN_RATE * direction).astype(jnp.bfloat16)
    second_sum = reduce_forward(partial_forward(new_weight))
    second_sum, new_left, new_right = lax.optimization_barrier((second_sum, new_left, new_right))
    second_out = lax.ppermute(second_sum, ALL, to_owner)
    return (first_out, new_left, new_right, direction, second_out)


def solution(mesh):
    in_specs = (
        P("batch", ("hidden", "solver")),
        P(("hidden", "solver"), "batch"),
        P(("hidden", "solver"), "batch"),
        P("hidden", "batch", None, None),
        P("hidden", "batch", None, None),
    )
    out_specs = (
        P(("hidden", "solver"), "batch"),
        P("hidden", "batch", "solver", None),
        P("hidden", "batch", "solver", None),
        P(("hidden", "solver"), "batch"),
        P(("hidden", "solver"), "batch"),
    )
    n_batch = mesh.shape["batch"]
    n_feat = mesh.shape["hidden"] * mesh.shape["solver"]

    def step(activations, cotangent, weight, left_old, right_old):
        return body(
            activations,
            cotangent,
            weight,
            left_old,
            right_old,
            n_batch=n_batch,
            n_solver=mesh.shape["solver"],
            n_feat=n_feat,
        )

    return jax.shard_map(step, mesh=mesh, in_specs=in_specs, out_specs=out_specs, check_vma=False)
```
